32 devices in a mesh: groups: 1, expert: 8 (over z, y), tensor: 2 (over x), pair: 2 (over core).
Axes of the slice: x: 2, y: 2, z: 4, core: 2. Of those that a mesh axis runs over, the one named last changes fastest.
Arguments:
- tokens: bfloat16 [512, 3584], P(('groups', 'expert', 'tensor', 'pair')), may hold values from -6 to 6
- expert_ids: int32 [512, 8], P(('groups', 'expert', 'tensor', 'pair')), may hold values from 0 to 15, all different within a row; in each aligned block of 16 rows (0 to 15, 16 to 31, ...) at most 16 rows name the same one
- route_weight: float32 [512, 8], P(('groups', 'expert', 'tensor', 'pair')), may hold values from 0.05 to 0.5
- w_gate: bfloat16 [16, 3584, 1024], P(('expert', 'pair'), None, 'tensor'), may hold values from -0.09375 to 0.09375
- w_up: bfloat16 [16, 3584, 1024], P(('expert', 'pair'), None, 'tensor'), may hold values from -0.09375 to 0.09375
- w_down: bfloat16 [16, 1024, 3584], P(('expert', 'pair'), 'tensor'), may hold values from -0.1875 to 0.1875
- s_gate: bfloat16 [3584, 2048], P(None, ('tensor', 'pair')), may hold values from -0.09375 to 0.09375
- s_up: bfloat16 [3584, 2048], P(None, ('tensor', 'pair')), may hold values from -0.09375 to 0.09375
- s_down: bfloat16 [2048, 3584], P(('tensor', 'pair')), may hold values from -0.125 to 0.125
Outputs:
- moe_out: bfloat16 [512, 3584], P(('groups', 'expert', 'tensor', 'pair'))
The draws below stay inside these ranges and needn't reach their ends.
Inputs may be any that keep to these rules, and one draw needn't show every extreme that they name: `expert_ids`: each row names 8 different experts. Among the 16 tokens of one device no expert is named by more than 16 tokens, and in every draw some expert is named by exactly 16 tokens of some device.
All inputs are finite; a program needn't handle non-finite values.
Results may differ from the reference program's by a relative error of at most 0.014.
Values may be sent and summed in bfloat16 or wider, within the bound.
A program may use at most 64 MiB of HBM per device.

```python
import math
import jax
import jax.numpy as jnp
import numpy as np
from jax import lax

D = 3584
EH = 1024
SH = 2048
TOP = 8
TOK_DEV = 16
EXPERTS = 16
CAP = 16
TOKENS = 512
N_EXPERT = 8
N_TENSOR = 2
N_PAIR = 2


def block_levels(key, dims, cuts, smallest, largest):
    level, own = 1.0, jax.random.fold_in(key, 6)
    for dim, parts in cuts:
        steps = jnp.exp(jax.random.uniform(jax.random.fold_in(own, dim), (parts,), jnp.float32, smallest / len(cuts), largest / len(cuts)))
        level = level * jnp.repeat(steps, dims[dim] // parts).reshape([-1 if axis == dim else 1 for axis in range(len(dims))])
    return level


def routed_block(rng, own, number, rows, amount, top, bound, slope):
    ranking = jax.random.permutation(rng, amount)
    heavy_load, ordinary = portions_of(amount, rows * top, bound, slope, True), portions_of(amount, rows * top, bound, slope, False)
    places = jnp.arange(amount)

    def named(lengths, turn):
        used = int((lengths > 0).sum())
        fixed = max(1, used // 4)
        passed = fixed + (places - fixed + turn * (used - fixed)) % max(1, amount - fixed)
        return jnp.zeros((amount,), jnp.int32).at[ranking[jnp.where(places < fixed, places, passed)]].set(jnp.asarray(lengths, jnp.int32))

    lengths = jnp.where(number % 4 == 0, named(heavy_load, number // 4), named(ordinary, number - number // 4 - 1))
    mixed = jax.random.permutation(jax.random.fold_in(own, 3), amount)
    donor, sink = mixed[0:amount // 2 * 2:2], mixed[1:amount // 2 * 2:2]
    room = jnp.minimum(lengths[donor] - 1, bound - lengths[sink]) // 2
    room = jnp.where((donor == ranking[0]) | (sink == ranking[0]) | (lengths[sink] == 0), 0, jnp.maximum(room, 0))
    passed = jax.random.randint(jax.random.fold_in(own, 4), (amount // 2,), 0, 1 << 20) % (room + 1)
    lengths = lengths.at[donor].add(-passed).at[sink].add(passed)
    items = jnp.searchsorted(jnp.cumsum(lengths), jnp.arange(rows * top), side="right").astype(jnp.int32)
    grid = items.reshape(top, rows).T
    grid = grid[jax.random.permutation(jax.random.fold_in(own, 1), rows)]
    turn = jax.random.randint(jax.random.fold_in(own, 2), (rows, 1), 0, top)
    return jnp.take_along_axis(grid, (jnp.arange(top)[None, :] + turn) % top, axis=1)


def portions_of(count, total, limit, lean, full):
    weights = [(1 << 20) // math.isqrt(standing ** lean) + 1 for standing in range(1, count + 1)]
    largest = limit if full else min(limit, max(-(-total // count), total * weights[0] // sum(weights)))
    least = 1 if total - largest >= count - 1 else 0
    holding, surplus = [largest] + [least] * (count - 1), total - largest - least * (count - 1)
    while surplus > 0:
        candidates = [i for i in range(1, count) if holding[i] < largest] or [i for i in range(1, count) if holding[i] < limit]
        mass, left = sum([weights[i] for i in candidates]), surplus
        for i in candidates:
            addition = min(limit - holding[i], max(1, left * weights[i] // mass), surplus)
            holding[i] = holding[i] + addition
            surplus = surplus - addition
    return np.array(holding)


def centred(own_key, shape, scale, limit, cuts=(), kind=jnp.bfloat16):
    values = scale * jax.random.normal(own_key, shape, jnp.float32)
    if cuts:
        values = values * block_levels(own_key, shape, cuts, -0.22, 0.18)
    return jnp.clip(values, -limit, limit).astype(kind)


def setup_inputs(seed: int = 0, part: int = 0) -> dict:
    key_of = jax.random.split(jax.random.key(seed), 10)
    part_splits = jax.random.split(jax.random.fold_in(key_of[9], part), 10)
    tokens = centred(part_splits[0], (TOKENS, D), 1.0, 6.0, ((0, 32),))
    expert_ids_keys = jax.random.split(jax.random.fold_in(part_splits[1], 1), TOKENS // TOK_DEV)
    expert_ids_turns = jax.random.permutation(jax.random.fold_in(part_splits[1], 3), TOKENS // TOK_DEV)
    expert_ids = jax.vmap(lambda own, number: routed_block(jax.random.fold_in(part_splits[1], 2), own, number, TOK_DEV, EXPERTS, TOP, CAP, 2))(expert_ids_keys, expert_ids_turns).reshape((TOKENS, TOP))
    route_weight = jnp.clip(0.05 + 0.45 * jax.random.uniform(part_splits[2], (TOKENS, TOP), jnp.float32) ** block_levels(part_splits[2], (TOKENS, TOP), ((0, 32),), -0.2, 0.2), 0.05, 0.5)
    w_gate = centred(key_of[3], (EXPERTS, D, EH), D ** -0.5, 0.09375, ((0, 16), (2, 2)))
    w_up = centred(key_of[4], (EXPERTS, D, EH), D ** -0.5, 0.09375, ((0, 16), (2, 2)))
    w_down = centred(key_of[5], (EXPERTS, EH, D), EH ** -0.5, 0.1875, ((0, 16), (1, 2)))
    s_gate = centred(key_of[6], (D, SH), D ** -0.5, 0.09375, ((1, 4),))
    s_up = centred(key_of[7], (D, SH), D ** -0.5, 0.09375, ((1, 4),))
    s_down = centred(key_of[8], (SH, D), SH ** -0.5, 0.125, ((0, 4),))
    return dict(tokens=tokens, expert_ids=expert_ids, route_weight=route_weight, w_gate=w_gate, w_up=w_up, w_down=w_down, s_gate=s_gate, s_up=s_up, s_down=s_down)


def reference(tokens, expert_ids, route_weight, w_gate, w_up, w_down, s_gate, s_up, s_down):
    highest = lax.Precision.HIGHEST
    tokens_wide = tokens.astype(jnp.float32)
    shared_gate = jnp.dot(tokens_wide, s_gate.astype(jnp.float32), precision=highest)
    shared_upper = jnp.dot(tokens_wide, s_up.astype(jnp.float32), precision=highest)
    shared_hidden = (jax.nn.silu(shared_gate) * shared_upper).astype(jnp.bfloat16)
    shared_hidden = lax.optimization_barrier(shared_hidden).astype(jnp.float32)
    shared = jnp.dot(shared_hidden, s_down.astype(jnp.float32), precision=highest)
    rows_most = min(TOKENS, N_EXPERT * N_TENSOR * N_PAIR * CAP)
    slice_width = EH // N_TENSOR

    def expert_step(total, expert):
        matches = expert_ids == expert
        coefficient = jnp.sum(jnp.where(matches, route_weight, 0.0), axis=1)
        chosen = jnp.any(matches, axis=1)
        row_order = jnp.argsort(jnp.where(chosen, 0, 1).astype(jnp.int32), stable=True)[:rows_most].astype(jnp.int32)
        picked = tokens_wide[row_order]
        gate_part = jnp.dot(picked, w_gate[expert].astype(jnp.float32), precision=highest)
        upper_part = jnp.dot(picked, w_up[expert].astype(jnp.float32), precision=highest)
        hidden = (jax.nn.silu(gate_part) * upper_part).astype(jnp.bfloat16)
        hidden = lax.optimization_barrier(hidden).astype(jnp.float32)
        down_rows = w_down[expert].astype(jnp.float32).reshape(N_TENSOR, slice_width, D)
        pieces = jnp.einsum("rjh,jhd->jrd", hidden.reshape(rows_most, N_TENSOR, slice_width), down_rows, precision=highest)
        pieces = lax.optimization_barrier(pieces.astype(jnp.bfloat16)).astype(jnp.float32)
        result = lax.optimization_barrier(jnp.sum(pieces, axis=0).astype(jnp.bfloat16)).astype(jnp.float32)
        total = total.at[row_order].add(result * coefficient[row_order][:, None])
        return total, None

    routed, _ = lax.scan(expert_step, jnp.zeros((TOKENS, D), jnp.float32), jnp.arange(EXPERTS, dtype=jnp.int32))
    return (shared + routed).astype(jnp.bfloat16)
```

```python
import functools

import jax
import jax.numpy as jnp
from jax import lax
from jax.experimental import pallas as pl
from jax.experimental.pallas import tpu as pltpu
from jax.sharding import PartitionSpec as P

MESH = pl.DeviceIdType.MESH
F32 = jnp.float32
BF16 = jnp.bfloat16


def lanes_for(experts):
    return -(-3 * experts // 128) * 128


def tile_of(width, most):
    for tile in range(min(width, most), 0, -1):
        if width % tile == 0 and (tile % 128 == 0 or tile == width):
            return tile
    return width


class Layout:
    def __init__(self, n_expert, n_tensor, n_pair, tok_rows):
        self.n_expert, self.n_tensor, self.n_pair = n_expert, n_tensor, n_pair
        self.ny = 2 if n_expert % 2 == 0 else 1
        self.nz = n_expert // self.ny
        self.swap = 1 if n_tensor == self.ny else 0
        self.na, self.nb = n_tensor, self.ny
        self.half = self.nz * self.na * self.nb
        self.blocks = 2 * self.half
        self.rows = tok_rows


def kernel(lay, experts, tok_in, ids, rw, wg_in, wu_in, wd_in, sg_in, su_in, sd_in, out,
           tok, part, recvp, recvb, recvl, recvr, recva, xs, hid, hs,
           wg, wu, wd, sg, su, sd, load_sem, tok_send, tok_recv, red_send, red_recv):
    nz, na, nb = lay.nz, lay.na, lay.nb
    rows, half = lay.rows, lay.half
    width = part.shape[-1]
    e_idx, t, p = lax.axis_index("expert"), lax.axis_index("tensor"), lax.axis_index("pair")
    z, y = e_idx // lay.ny, e_idx % lay.ny
    s = p * lay.swap
    a = t * (1 - s) + y * s
    b = y * (1 - s) + t * s

    def device(z_, b_, a_):
        t_ = a_ * (1 - s) + b_ * s
        y_ = b_ * (1 - s) + a_ * s
        return {"expert": z_ * lay.ny + y_, "tensor": t_, "pair": p}

    partner = {"expert": e_idx, "tensor": t, "pair": 1 - p}
    a_peers = [(a + d) % na for d in range(1, na)]
    b_peers = [(b + d) % nb for d in range(1, nb)]

    def place(q, z_, b_, a_):
        return ((q * nz + z_) * nb + b_) * na + a_

    own = place(p, z, b, a)
    first = pltpu.make_async_copy(tok_in, tok.at[own, :, pl.ds(0, width)], load_sem.at[6])
    first.start()
    loads = [
        pltpu.make_async_copy(src, dst, load_sem.at[i])
        for i, (src, dst) in enumerate(
            ((sg_in, sg), (su_in, su), (sd_in, sd), (wg_in.at[0], wg), (wu_in.at[0], wu), (wd_in.at[0], wd))
        )
    ]
    for load in loads:
        load.start()

    barrier = pltpu.get_barrier_semaphore()

    def greet(dev):
        pl.semaphore_signal(barrier, inc=1, device_id=dev, device_id_type=MESH)

    greet(partner)
    for a_ in a_peers:
        greet(device(z, b, a_))
    for b_ in b_peers:
        greet(device(z, b_, a))
    up, down = z < nz - 1, z > 0

    @pl.when(up)
    def _():
        greet(device(z + 1, b, a))

    @pl.when(down)
    def _():
        greet(device(z - 1, b, a))

    lane = lax.broadcasted_iota(jnp.int32, (rows, tok.shape[-1] - width), 1)
    top = ids.shape[1]
    pieces = [jnp.zeros(lane.shape, F32) for _ in range(3)]
    for k in range(top):
        for m in range(3):
            pieces[m] = pieces[m] + jnp.where(lane == ids[:, k : k + 1] + m * experts, rw[:, k : k + 1], 0.0)
    hi = [v.astype(BF16).astype(F32) for v in pieces]
    rest = [v - h for v, h in zip(pieces, hi)]
    mid = [v.astype(BF16).astype(F32) for v in rest]
    low = [v - h for v, h in zip(rest, mid)]
    tok[own, :, pl.ds(width, lane.shape[1])] = (hi[0] + mid[1] + low[2]).astype(BF16)

    line_peers = jnp.minimum(z, 1) + jnp.minimum(nz - 1 - z, 1)
    pl.semaphore_wait(barrier, na + nb - 1 + line_peers)

    first.wait()

    sent = []

    def both(c1, c2):
        return c2 if c1 is None else (c1 if c2 is None else jnp.logical_and(c1, c2))

    def run(cond, fn):
        if cond is None:
            fn()
        else:
            pl.when(cond)(fn)

    def send(src, dst, sem_send, sem_recv, dev, cond=None):
        copy = pltpu.make_async_remote_copy(
            src_ref=src, dst_ref=dst, send_sem=sem_send, recv_sem=sem_recv,
            device_id=dev, device_id_type=MESH)
        run(cond, copy.start)
        sent.append((cond, copy))

    counter = [0]

    def send_block(idx, dev, cond=None):
        send(tok.at[idx], tok.at[idx], tok_send.at[counter[0]], tok_recv.at[idx], dev, cond)
        counter[0] += 1

    def arrive(idx, cond=None):
        copy = pltpu.make_async_remote_copy(
            src_ref=tok.at[idx], dst_ref=tok.at[idx], send_sem=tok_send.at[0],
            recv_sem=tok_recv.at[idx], device_id=partner, device_id_type=MESH)
        run(cond, copy.wait_recv)

    for a_ in a_peers:
        send_block(own, device(z, b, a_))
    for k in range(nz):
        for step, a_ in enumerate([a] + a_peers):
            for sign in ((1, -1) if k else (0,)):
                z_ = z + sign * k
                cond = None if sign == 0 else (z_ < nz if sign > 0 else z_ >= 0)
                blk = place(p, z_, b, a_)
                if k or step:
                    arrive(blk, cond)
                if sign <= 0:
                    send_block(blk, device(z + 1, b, a), both(cond, up))
                if sign >= 0:
                    send_block(blk, device(z - 1, b, a), both(cond, down))
                for b_ in b_peers:
                    send_block(blk, device(z, b_, a), cond)
                send_block(blk, partner, cond)
    for k in range(nz):
        for b_ in b_peers:
            for a_ in [a] + a_peers:
                for sign in ((1, -1) if k else (0,)):
                    z_ = z + sign * k
                    cond = None if sign == 0 else (z_ < nz if sign > 0 else z_ >= 0)
                    blk = place(p, z_, b_, a_)
                    arrive(blk, cond)
                    send_block(blk, partner, cond)
    for z_ in range(nz):
        for b_ in range(nb):
            for a_ in range(na):
                arrive(place(1 - p, z_, b_, a_))

    group = []
    for q in range(2):
        for t_ in range(lay.n_tensor):
            sq = q * lay.swap
            group.append(place(q, z, t_ if sq else y, y if sq else t_))
    for i, idx in enumerate(group):
        xs[i] = tok[idx, :, pl.ds(0, width)]
    count = len(group)

    def hidden_tiles(x, w1, w2, scale, store):
        tile = tile_of(w1.shape[1], 256)

        def body(n, _):
            cols = pl.ds(pl.multiple_of(n * tile, tile), tile)
            g = jnp.dot(x(), w1[:, cols], preferred_element_type=F32)
            u = jnp.dot(x(), w2[:, cols], preferred_element_type=F32)
            h = g / (1.0 + jnp.exp(-g)) * u
            if scale is not None:
                h = h * scale
            store[:, cols] = h.astype(BF16)
            return 0

        lax.fori_loop(0, w1.shape[1] // tile, body, 0)

    loads[0].wait()
    loads[1].wait()
    hidden_tiles(lambda: xs[...].reshape(count * rows, width), sg, su, None, hs)
    loads[2].wait()
    for i in range(3, 6):
        loads[i].wait()

    out_tile = tile_of(width, 512)
    per = min(half, max(1, 256 // rows))
    while half % per:
        per -= 1
    mine = e_idx * lay.n_pair + p

    def chunk(c, _):
        at = c * per
        extra = tok[pl.ds(at, per), :, pl.ds(width, lane.shape[1])].reshape(per * rows, lane.shape[1])
        l2 = lax.broadcasted_iota(jnp.int32, extra.shape, 1)
        pick = (l2 == mine) | (l2 == mine + experts) | (l2 == mine + 2 * experts)
        scale = jnp.sum(jnp.where(pick, extra.astype(F32), 0.0), axis=1, keepdims=True)
        hidden_tiles(lambda: tok[pl.ds(at, per), :, pl.ds(0, width)].reshape(per * rows, width), wg, wu, scale, hid)

        def body(n, _):
            cols = pl.ds(pl.multiple_of(n * out_tile, out_tile), out_tile)
            v = jnp.dot(hid[...], wd[:, cols], preferred_element_type=F32)
            part[pl.ds(at, per), :, cols] = v.astype(BF16).reshape(per, rows, out_tile)
            return 0

        lax.fori_loop(0, width // out_tile, body, 0)
        return 0

    def shared_into(q):
        lo = q * (count // 2)

        def body(n, _):
            cols = pl.ds(pl.multiple_of(n * out_tile, out_tile), out_tile)
            r0 = pl.multiple_of(lo * rows, rows)
            v = jnp.dot(hs[pl.ds(r0, count // 2 * rows), :], sd[:, cols], preferred_element_type=F32)
            for j in range(count // 2):
                sq = q * lay.swap
                idx = place(q, z, j * sq + y * (1 - sq), y * sq + j * (1 - sq))
                part[idx, :, cols] = (part[idx, :, cols].astype(F32) + v[j * rows : (j + 1) * rows]).astype(BF16)
            return 0

        lax.fori_loop(0, width // out_tile, body, 0)

    rcount = [0]

    def send_sum(src, dst, recv_at, dev, cond=None):
        send(src, dst, red_send.at[rcount[0]], red_recv.at[recv_at], dev, cond)
        rcount[0] += 1

    def got(dst, recv_at, cond=None):
        copy = pltpu.make_async_remote_copy(
            src_ref=dst, dst_ref=dst, send_sem=red_send.at[0], recv_sem=red_recv.at[recv_at],
            device_id=partner, device_id_type=MESH)
        run(cond, copy.wait_recv)

    steps = half // per
    other = 1 - p
    lax.fori_loop(0, steps, lambda c, v: chunk(other * steps + c, v), 0)
    shared_into(other)

    def line_order():
        order = []
        for k in range(nz - 1, 0, -1):
            order += [(z + k, z + k < nz, 1), (z - k, z - k >= 0, -1)]
        return order + [(z, None, 0)]

    def p_slot(z_, b_):
        return z_ * nb + b_

    base_b = nz * nb
    base_l = base_b + (nb - 1) * nz
    base_r = base_l + nz
    base_a = base_r + nz

    def piece(q, z_, b_):
        return part.at[pl.ds(place(q, z_, b_, 0), na)]

    for b_ in list(range(nb)):
        for z_ in range(nz):
            slot = p_slot(z_, b_)
            send_sum(piece(other, z_, b_), recvp.at[slot], slot, partner)
    lax.fori_loop(0, steps, lambda c, v: chunk(p * steps + c, v), 0)
    shared_into(p)

    def add_into(q, z_, b_, others, cond):
        def fn():
            def blk(i, _):
                idx = place(q, z_, b_, i)
                v = part[idx].astype(F32)
                for ref in others:
                    v = v + ref[i].astype(F32)
                part[idx] = v.astype(BF16)
                return 0
            lax.fori_loop(0, na, blk, 0)
        run(cond, fn)

    for z_, cond, sign in line_order():
        for d, b_ in enumerate(b_peers):
            got(recvp.at[p_slot(z_, b_)], p_slot(z_, b_), cond)
            add_into(p, z_, b_, [recvp.at[p_slot(z_, b_)]], cond)
            send_sum(piece(p, z_, b_), recvb.at[d * nz + z_], base_b + d * nz + z_, device(z, b_, a), cond)
    for z_, cond, sign in line_order():
        got(recvp.at[p_slot(z_, b)], p_slot(z_, b), cond)
        others = [recvp.at[p_slot(z_, b)]]
        for d in range(nb - 1):
            got(recvb.at[d * nz + z_], base_b + d * nz + z_, cond)
            others.append(recvb.at[d * nz + z_])
        add_into(p, z_, b, others, cond)
        if sign >= 0:
            got(recvl.at[z_], base_l + z_, both(cond, down))
            add_into(p, z_, b, [recvl.at[z_]], both(cond, down))
        if sign <= 0:
            got(recvr.at[z_], base_r + z_, both(cond, up))
            add_into(p, z_, b, [recvr.at[z_]], both(cond, up))
        if sign > 0:
            send_sum(piece(p, z_, b), recvl.at[z_], base_l + z_, device(z + 1, b, a), cond)
        if sign < 0:
            send_sum(piece(p, z_, b), recvr.at[z_], base_r + z_, device(z - 1, b, a), cond)
    for d, a_ in enumerate(a_peers):
        send_sum(part.at[place(p, z, b, a_)], recva.at[d], base_a + d, device(z, b, a_))
    total = part[own].astype(F32)
    for d in range(na - 1):
        got(recva.at[d], base_a + d)
        total = total + recva[d].astype(F32)
    out[...] = total.astype(BF16)
    for cond, copy in sent:
        run(cond, copy.wait_send)


def per_device(lay, experts, tokens, ids, rw, wg, wu, wd, sg, su, sd):
    rows, width = tokens.shape
    nz, na, nb = lay.nz, lay.na, lay.nb
    piece = (na, rows, width)
    count = 2 * lay.n_tensor
    hidden, shared = wg.shape[2], sg.shape[1]
    per = min(lay.half, max(1, 256 // rows))
    while lay.half % per:
        per -= 1
    sends = (na - 1) + (na * (2 * nz - 1)) * (2 + nb) + (nb - 1) * na * (2 * nz - 1) + 8
    red = nz * nb + (2 * nz - 1) * nb + 2 * nz + na + 8
    vmem = pl.BlockSpec(memory_space=pltpu.VMEM)
    anyw = pl.BlockSpec(memory_space=pl.ANY)
    scratch = [
        pltpu.VMEM((lay.blocks, rows, width + lanes_for(experts)), BF16),
        pltpu.VMEM((lay.blocks, rows, width), BF16),
        pltpu.VMEM((nz * nb,) + piece, BF16),
        pltpu.VMEM((max(1, (nb - 1) * nz),) + piece, BF16),
        pltpu.VMEM((nz,) + piece, BF16),
        pltpu.VMEM((nz,) + piece, BF16),
        pltpu.VMEM((max(1, na - 1), rows, width), BF16),
        pltpu.VMEM((count, rows, width), BF16),
        pltpu.VMEM((per * rows, hidden), BF16),
        pltpu.VMEM((count * rows, shared), BF16),
        pltpu.VMEM(wg.shape[1:], BF16),
        pltpu.VMEM(wu.shape[1:], BF16),
        pltpu.VMEM(wd.shape[1:], BF16),
        pltpu.VMEM(sg.shape, BF16),
        pltpu.VMEM(su.shape, BF16),
        pltpu.VMEM(sd.shape, BF16),
        pltpu.SemaphoreType.DMA((7,)),
        pltpu.SemaphoreType.DMA((sends,)),
        pltpu.SemaphoreType.DMA((lay.blocks,)),
        pltpu.SemaphoreType.DMA((red,)),
        pltpu.SemaphoreType.DMA((nz * nb + (nb - 1) * nz + 2 * nz + na,)),
    ]
    return pl.pallas_call(
        functools.partial(kernel, lay, experts),
        out_shape=jax.ShapeDtypeStruct((rows, width), BF16),
        in_specs=[anyw, vmem, vmem] + [anyw] * 6,
        out_specs=vmem,
        scratch_shapes=scratch,
        compiler_params=pltpu.CompilerParams(
            collective_id=0, has_side_effects=True, vmem_limit_bytes=67043328
        ),
    )(tokens, ids, rw, wg, wu, wd, sg, su, sd)


def solution(mesh):
    shape = dict(mesh.shape)

    def body(tokens, ids, rw, wg, wu, wd, sg, su, sd):
        lay = Layout(shape["expert"], shape["tensor"], shape["pair"], tokens.shape[0])
        experts = shape["expert"] * shape["pair"] * wg.shape[0]
        return per_device(lay, experts, tokens, ids, rw, wg, wu, wd, sg, su, sd)

    in_specs = (
        P(("groups", "expert", "tensor", "pair"), None),
        P(("groups", "expert", "tensor", "pair"), None),
        P(("groups", "expert", "tensor", "pair"), None),
        P(("expert", "pair"), None, "tensor"),
        P(("expert", "pair"), None, "tensor"),
        P(("expert", "pair"), "tensor", None),
        P(None, ("tensor", "pair")),
        P(None, ("tensor", "pair")),
        P(("tensor", "pair"), None),
    )
    out_specs = P(("groups", "expert", "tensor", "pair"), None)
    return jax.shard_map(body, mesh=mesh, in_specs=in_specs, out_specs=out_specs, check_vma=False)
```

```python
import functools

import jax
import jax.numpy as jnp
from jax import lax
from jax.experimental import pallas as pl
from jax.experimental.pallas import tpu as pltpu
from jax.sharding import PartitionSpec as P

MESH = pl.DeviceIdType.MESH
F32 = jnp.float32
BF16 = jnp.bfloat16


def lanes_for(experts):
    return -(-3 * experts // 128) * 128


def tile_of(width, most):
    for tile in range(min(width, most), 0, -1):
        if width % tile == 0 and (tile % 128 == 0 or tile == width):
            return tile
    return width


class Layout:
    def __init__(self, n_expert, n_tensor, n_pair, tok_rows):
        self.n_expert, self.n_tensor, self.n_pair = n_expert, n_tensor, n_pair
        self.ny = 2 if n_expert % 2 == 0 else 1
        self.nz = n_expert // self.ny
        self.half = n_expert * n_tensor
        self.blocks = 2 * self.half
        self.rows = tok_rows
        self.first = (n_tensor, self.ny)
        self.last = (self.ny, n_tensor)

    def steps(self, z):
        out = [[(z, None)]]
        for k in range(1, self.nz):
            out.append([(z + k, z + k < self.nz), (z - k, z - k >= 0)])
        return out


def kernel(lay, experts, tok_in, ids_in, rw_in, wg_in, wu_in, wd_in, sg_in, su_in, sd_in, out,
           tok, part, ids, rw, recvp, recvb0, recvb1, recva0, recva1, recvz, xs, hid, hs,
           wg, wu, wd, sg, su, sd, load_sem, tok_send, tok_recv, red_send, red_recv):
    nz, ny, nt = lay.nz, lay.ny, lay.n_tensor
    rows, half = lay.rows, lay.half
    width = part.shape[-1]
    e_idx, t, p = lax.axis_index("expert"), lax.axis_index("tensor"), lax.axis_index("pair")
    z, y = e_idx // ny, e_idx % ny

    def device(z_, y_, t_):
        return {"expert": z_ * ny + y_, "tensor": t_, "pair": p}

    partner = {"expert": e_idx, "tensor": t, "pair": 1 - p}
    t_peers = [(t + d) % nt for d in range(1, nt)]
    y_peers = [(y + d) % ny for d in range(1, ny)]
    z_peers = [(z + d) % nz for d in range(1, nz)]

    def place(q, z_, y_, t_):
        return ((q * nz + z_) * ny + y_) * nt + t_

    cut = width // 256 * 128
    wide = (pl.ds(0, cut), pl.ds(cut, tok.shape[-1] - cut))
    cols2 = (pl.ds(0, cut), pl.ds(cut, width - cut))
    first_peers, last_peers = (t_peers, y_peers), (y_peers, t_peers)
    first_at, last_at = (t, y), (y, t)

    def yt(h, first_, last_):
        return (last_, first_) if h == 0 else (first_, last_)

    own = place(p, z, y, t)
    first = pltpu.make_async_copy(tok_in, tok.at[own, :, pl.ds(0, width)], load_sem.at[6])
    first.start()
    small = [pltpu.make_async_copy(ids_in, ids, load_sem.at[7]), pltpu.make_async_copy(rw_in, rw, load_sem.at[8])]
    for load in small:
        load.start()
    loads = [
        pltpu.make_async_copy(src, dst, load_sem.at[i])
        for i, (src, dst) in enumerate(
            ((sg_in, sg), (su_in, su), (sd_in, sd), (wg_in.at[0], wg), (wu_in.at[0], wu), (wd_in.at[0], wd))
        )
    ]
    for load in loads:
        load.start()

    barrier = pltpu.get_barrier_semaphore()

    def greet(dev):
        pl.semaphore_signal(barrier, inc=1, device_id=dev, device_id_type=MESH)

    greet(partner)
    for t_ in t_peers:
        greet(device(z, y, t_))
    for y_ in y_peers:
        greet(device(z, y_, t))
    for z_ in z_peers:
        greet(device(z_, y, t))

    for load in small:
        load.wait()
    lane = lax.broadcasted_iota(jnp.int32, (rows, tok.shape[-1] - width), 1)
    top = ids.shape[1]
    pieces = [jnp.zeros(lane.shape, F32) for _ in range(3)]
    for k in range(top):
        for m in range(3):
            pieces[m] = pieces[m] + jnp.where(lane == ids[:, k : k + 1] + m * experts, rw[:, k : k + 1], 0.0)
    hi = [v.astype(BF16).astype(F32) for v in pieces]
    rest = [v - h for v, h in zip(pieces, hi)]
    mid = [v.astype(BF16).astype(F32) for v in rest]
    low = [v - h for v, h in zip(rest, mid)]
    tok[own, :, pl.ds(width, lane.shape[1])] = (hi[0] + mid[1] + low[2]).astype(BF16)

    pl.semaphore_wait(barrier, nt + ny + nz - 2)

    first.wait()

    sent = []

    def both(c1, c2):
        return c2 if c1 is None else (c1 if c2 is None else jnp.logical_and(c1, c2))

    def run(cond, fn):
        if cond is None:
            fn()
        else:
            pl.when(cond)(fn)

    def send(src, dst, sem_send, sem_recv, dev, cond=None):
        copy = pltpu.make_async_remote_copy(
            src_ref=src, dst_ref=dst, send_sem=sem_send, recv_sem=sem_recv,
            device_id=dev, device_id_type=MESH)
        run(cond, copy.start)
        sent.append((cond, copy))

    counter = [0]

    def send_block(h, idx, dev, cond=None):
        view = tok.at[idx, :, wide[h]]
        send(view, view, tok_send.at[counter[0]], tok_recv.at[h, idx], dev, cond)
        counter[0] += 1

    def arrive(h, idx, cond=None):
        view = tok.at[idx, :, wide[h]]
        copy = pltpu.make_async_remote_copy(
            src_ref=view, dst_ref=view, send_sem=tok_send.at[0],
            recv_sem=tok_recv.at[h, idx], device_id=partner, device_id_type=MESH)
        run(cond, copy.wait_recv)

    def last_sends(h, idx, cond):
        for v in last_peers[h]:
            send_block(h, idx, device(z, *yt(h, first_at[h], v)), cond)

    def stage_line(k):
        for z_, cond in line[k]:
            blk = place(p, z_, y, t)
            for h in range(2):
                if k:
                    arrive(h, blk, cond)
                for v in first_peers[h]:
                    send_block(h, blk, device(z, *yt(h, v, last_at[h])), cond)
            for h in range(2):
                last_sends(h, blk, cond)
                send_block(h, blk, partner, cond)

    def stage_first(k):
        for z_, cond in line[k]:
            for d in range(max(ny, nt) - 1):
                for h in range(2):
                    if d < len(first_peers[h]):
                        blk = place(p, z_, *yt(h, first_peers[h][d], last_at[h]))
                        arrive(h, blk, cond)
                        last_sends(h, blk, cond)
                        send_block(h, blk, partner, cond)

    def stage_last(k):
        for z_, cond in line[k]:
            for h in range(2):
                for f in [first_at[h]] + first_peers[h]:
                    for v in last_peers[h]:
                        blk = place(p, z_, *yt(h, f, v))
                        arrive(h, blk, cond)
                        send_block(h, blk, partner, cond)

    line = lay.steps(z)
    for k in range(1, nz):
        for z_, cond in line[k]:
            for h in range(2):
                send_block(h, own, device(z_, y, t), cond)
    for k in range(nz + 2):
        if k < nz:
            stage_line(k)
        if 0 <= k - 1 < nz:
            stage_first(k - 1)
        if 0 <= k - 2 < nz:
            stage_last(k - 2)
    for k in range(nz):
        for z_, cond in line[k]:
            for y_ in range(ny):
                for t_ in range(nt):
                    for h in range(2):
                        arrive(h, place(1 - p, z_, y_, t_), cond)

    group = []
    for q in range(2):
        for t_ in range(lay.n_tensor):
            group.append(place(q, z, y, t_))
    for i, idx in enumerate(group):
        xs[i] = tok[idx, :, pl.ds(0, width)]
    count = len(group)

    def hidden_tiles(x, w1, w2, scale, store):
        tile = tile_of(w1.shape[1], 256)

        def body(n, _):
            cols = pl.ds(pl.multiple_of(n * tile, tile), tile)
            g = jnp.dot(x(), w1[:, cols], preferred_element_type=F32)
            u = jnp.dot(x(), w2[:, cols], preferred_element_type=F32)
            h = g / (1.0 + jnp.exp(-g)) * u
            if scale is not None:
                h = h * scale
            store[:, cols] = h.astype(BF16)
            return 0

        lax.fori_loop(0, w1.shape[1] // tile, body, 0)

    loads[0].wait()
    loads[1].wait()
    hidden_tiles(lambda: xs[...].reshape(count * rows, width), sg, su, None, hs)
    loads[2].wait()
    for i in range(3, 6):
        loads[i].wait()

    out_tile = tile_of(width, 512)
    per = min(half, max(1, 256 // rows))
    while half % per:
        per -= 1
    mine = e_idx * lay.n_pair + p

    def chunk(c, _):
        at = c * per
        extra = tok[pl.ds(at, per), :, pl.ds(width, lane.shape[1])].reshape(per * rows, lane.shape[1])
        l2 = lax.broadcasted_iota(jnp.int32, extra.shape, 1)
        pick = (l2 == mine) | (l2 == mine + experts) | (l2 == mine + 2 * experts)
        scale = jnp.sum(jnp.where(pick, extra.astype(F32), 0.0), axis=1, keepdims=True)
        hidden_tiles(lambda: tok[pl.ds(at, per), :, pl.ds(0, width)].reshape(per * rows, width), wg, wu, scale, hid)

        def body(n, _):
            cols = pl.ds(pl.multiple_of(n * out_tile, out_tile), out_tile)
            v = jnp.dot(hid[...], wd[:, cols], preferred_element_type=F32)
            part[pl.ds(at, per), :, cols] = v.astype(BF16).reshape(per, rows, out_tile)
            return 0

        lax.fori_loop(0, width // out_tile, body, 0)
        return 0

    def shared_into(q):
        lo = q * (count // 2)

        def body(n, _):
            cols = pl.ds(pl.multiple_of(n * out_tile, out_tile), out_tile)
            r0 = pl.multiple_of(lo * rows, rows)
            v = jnp.dot(hs[pl.ds(r0, count // 2 * rows), :], sd[:, cols], preferred_element_type=F32)
            for j in range(count // 2):
                idx = place(q, z, y, j)
                part[idx, :, cols] = (part[idx, :, cols].astype(F32) + v[j * rows : (j + 1) * rows]).astype(BF16)
            return 0

        lax.fori_loop(0, width // out_tile, body, 0)

    rcount = [0]

    def send_sum(src, dst, recv_at, dev, cond=None):
        send(src, dst, red_send.at[rcount[0]], red_recv.at[recv_at], dev, cond)
        rcount[0] += 1

    def got(dst, recv_at, cond=None):
        copy = pltpu.make_async_remote_copy(
            src_ref=dst, dst_ref=dst, send_sem=red_send.at[0], recv_sem=red_recv.at[recv_at],
            device_id=partner, device_id_type=MESH)
        run(cond, copy.wait_recv)

    steps = half // per
    other = 1 - p
    lax.fori_loop(0, steps, lambda c, v: chunk(other * steps + c, v), 0)
    shared_into(other)

    recvb, recva = (recvb0, recvb1), (recva0, recva1)
    base = [half]
    bases = {}

    def at(kind, h, n):
        if (kind, h) not in bases:
            bases[kind, h] = base[0]
            base[0] += n
        return bases[kind, h]

    far = [pair for k in range(nz - 1, -1, -1) for pair in line[k]]

    for y_ in range(ny):
        for z_ in range(nz):
            at_ = z_ * ny + y_
            send_sum(part.at[pl.ds(place(other, z_, y_, 0), nt)], recvp.at[pl.ds(at_ * nt, nt)], at_, partner)
    lax.fori_loop(0, steps, lambda c, v: chunk(p * steps + c, v), 0)
    shared_into(p)

    def buf_b(h, d, z_, f):
        n = lay.first[h]
        at_ = (d * nz + z_) * n + f
        return recvb[h].at[at_], at("b", h, (lay.last[h] - 1) * nz * n) + at_

    def buf_a(h, d, z_):
        return recva[h].at[d * nz + z_], at("a", h, (lay.first[h] - 1) * nz) + d * nz + z_

    def buf_z(h, d):
        return recvz.at[d, :, cols2[h]], at("z", h, nz - 1) + d

    def add_into(h, idx, others, cond):
        def fn():
            v = part[idx, :, cols2[h]].astype(F32)
            for ref in others:
                v = v + ref[...].astype(F32)
            part[idx, :, cols2[h]] = v.astype(BF16)
        run(cond, fn)

    def mine_of(z_, y_, t_, h):
        return recvp.at[(z_ * ny + y_) * nt + t_, :, cols2[h]]

    def sums_last(z_, cond):
        for y_ in [(y + 1 + d) % ny for d in range(ny)]:
            got(recvp.at[pl.ds((z_ * ny + y_) * nt, nt)], z_ * ny + y_, cond)
        for f in range(max(ny, nt) - 1, -1, -1):
            for h in range(2):
                firsts = [first_at[h]] + first_peers[h]
                if f >= len(firsts):
                    continue
                for d, v in enumerate(last_peers[h]):
                    y_, t_ = yt(h, firsts[f], v)
                    idx = place(p, z_, y_, t_)
                    add_into(h, idx, [mine_of(z_, y_, t_, h)], cond)
                    ref, sem = buf_b(h, d, z_, firsts[f])
                    y2, t2 = yt(h, first_at[h], v)
                    send_sum(part.at[idx, :, cols2[h]], ref, sem, device(z, y2, t2), cond)

    def collect_last(h, z_, f, cond):
        y_, t_ = yt(h, f, last_at[h])
        refs = [mine_of(z_, y_, t_, h)]
        for d in range(lay.last[h] - 1):
            ref, sem = buf_b(h, d, z_, f)
            got(ref, sem, cond)
            refs.append(ref)
        return place(p, z_, y_, t_), refs

    def sums_first(z_, cond):
        for h in range(2):
            for d, f in enumerate(first_peers[h]):
                idx, refs = collect_last(h, z_, f, cond)
                add_into(h, idx, refs, cond)
                ref, sem = buf_a(h, d, z_)
                send_sum(part.at[idx, :, cols2[h]], ref, sem, device(z, *yt(h, f, last_at[h])), cond)

    def sums_line(z_, cond):
        for h in range(2):
            idx, refs = collect_last(h, z_, first_at[h], cond)
            for d in range(lay.first[h] - 1):
                ref, sem = buf_a(h, d, z_)
                got(ref, sem, cond)
                refs.append(ref)
            if cond is None:
                for d in range(nz - 1):
                    ref, sem = buf_z(h, d)
                    got(ref, sem)
                    refs.append(ref)
            add_into(h, idx, refs, cond)
            if cond is not None:
                d = (z_ - z + nz) % nz - 1
                ref, sem = buf_z(h, d)
                send_sum(part.at[idx, :, cols2[h]], ref, sem, device(z_, y, t), cond)

    for i in range(len(far) + 4):
        if i < len(far):
            sums_last(*far[i])
        if 0 <= i - 2 < len(far):
            sums_first(*far[i - 2])
        if 0 <= i - 4 < len(far):
            sums_line(*far[i - 4])
    total = part[own]
    out[...] = total
    for cond, copy in sent:
        run(cond, copy.wait_send)


def per_device(lay, experts, tokens, ids, rw, wg, wu, wd, sg, su, sd):
    rows, width = tokens.shape
    nz, ny, nt = lay.nz, lay.ny, lay.n_tensor
    cut = width // 256 * 128
    count = 2 * lay.n_tensor
    hidden, shared = wg.shape[2], sg.shape[1]
    per = min(lay.half, max(1, 256 // rows))
    while lay.half % per:
        per -= 1
    span = 2 * nz - 1
    sends = 4 * (nz - 1) + span * (nt - 1 + ny - 1) + 2 * span * (nt * ny) + span * 2 * nt * ny
    red = nz * ny + 2 * span * nt * ny + 4 * nz + 2 * span * (nt + ny)
    halves = (cut, width - cut)
    many_b = [max(1, (lay.last[h] - 1) * nz * lay.first[h]) for h in range(2)]
    many_a = [max(1, (lay.first[h] - 1) * nz) for h in range(2)]
    vmem = pl.BlockSpec(memory_space=pltpu.VMEM)
    anyw = pl.BlockSpec(memory_space=pl.ANY)
    scratch = [
        pltpu.VMEM((lay.blocks, rows, width + lanes_for(experts)), BF16),
        pltpu.VMEM((lay.blocks, rows, width), BF16),
        pltpu.VMEM(ids.shape, jnp.int32),
        pltpu.VMEM(rw.shape, F32),
        pltpu.VMEM((lay.half, rows, width), BF16),
        pltpu.VMEM((many_b[0], rows, halves[0]), BF16),
        pltpu.VMEM((many_b[1], rows, halves[1]), BF16),
        pltpu.VMEM((many_a[0], rows, halves[0]), BF16),
        pltpu.VMEM((many_a[1], rows, halves[1]), BF16),
        pltpu.VMEM((max(1, nz - 1), rows, width), BF16),
        pltpu.VMEM((count, rows, width), BF16),
        pltpu.VMEM((per * rows, hidden), BF16),
        pltpu.VMEM((count * rows, shared), BF16),
        pltpu.VMEM(wg.shape[1:], BF16),
        pltpu.VMEM(wu.shape[1:], BF16),
        pltpu.VMEM(wd.shape[1:], BF16),
        pltpu.VMEM(sg.shape, BF16),
        pltpu.VMEM(su.shape, BF16),
        pltpu.VMEM(sd.shape, BF16),
        pltpu.SemaphoreType.DMA((9,)),
        pltpu.SemaphoreType.DMA((sends,)),
        pltpu.SemaphoreType.DMA((2, lay.blocks)),
        pltpu.SemaphoreType.DMA((red,)),
        pltpu.SemaphoreType.DMA((lay.half + sum(many_b) + sum(many_a) + 2 * nz,)),
    ]
    return pl.pallas_call(
        functools.partial(kernel, lay, experts),
        out_shape=jax.ShapeDtypeStruct((rows, width), BF16),
        in_specs=[anyw] * 9,
        out_specs=vmem,
        scratch_shapes=scratch,
        compiler_params=pltpu.CompilerParams(
            collective_id=0, has_side_effects=True, vmem_limit_bytes=67043328
        ),
    )(tokens, ids, rw, wg, wu, wd, sg, su, sd)


def solution(mesh):
    shape = dict(mesh.shape)

    def body(tokens, ids, rw, wg, wu, wd, sg, su, sd):
        lay = Layout(shape["expert"], shape["tensor"], shape["pair"], tokens.shape[0])
        experts = shape["expert"] * shape["pair"] * wg.shape[0]
        return per_device(lay, experts, tokens, ids, rw, wg, wu, wd, sg, su, sd)

    in_specs = (
        P(("groups", "expert", "tensor", "pair"), None),
        P(("groups", "expert", "tensor", "pair"), None),
        P(("groups", "expert", "tensor", "pair"), None),
        P(("expert", "pair"), None, "tensor"),
        P(("expert", "pair"), None, "tensor"),
        P(("expert", "pair"), "tensor", None),
        P(None, ("tensor", "pair")),
        P(None, ("tensor", "pair")),
        P(("tensor", "pair"), None),
    )
    out_specs = P(("groups", "expert", "tensor", "pair"), None)
    return jax.shard_map(body, mesh=mesh, in_specs=in_specs, out_specs=out_specs, check_vma=False)
```

```python
import functools

import jax
import jax.numpy as jnp
from jax import lax
from jax.experimental import pallas as pl
from jax.experimental.pallas import tpu as pltpu
from jax.sharding import PartitionSpec as P

MESH = pl.DeviceIdType.MESH
F32 = jnp.float32
BF16 = jnp.bfloat16


def lanes_for(experts):
    return -(-3 * experts // 128) * 128


def tile_of(width, most):
    for tile in range(min(width, most), 0, -1):
        if width % tile == 0 and (tile % 128 == 0 or tile == width):
            return tile
    return width


def part_rows(span, rows):
    per = min(span, max(1, 256 // rows))
    while span % per:
        per -= 1
    return per


class Layout:
    def __init__(self, n_expert, n_tensor, n_pair, tok_rows):
        self.n_expert, self.n_tensor, self.n_pair = n_expert, n_tensor, n_pair
        self.ny = 2 if n_expert % 2 == 0 else 1
        self.nz = n_expert // self.ny
        self.half = n_expert * n_tensor
        self.blocks = 2 * self.half
        self.rows = tok_rows
        self.first = (n_tensor, self.ny)
        self.last = (self.ny, n_tensor)

    def near_far(self, z):
        if self.nz % 2:
            return [z] + [(z + d) % self.nz for d in range(1, self.nz)], []
        hz = self.nz // 2
        zh = z // hz
        near = [z] + [zh * hz + (z + d) % hz for d in range(1, hz)]
        far = [(hz + d) * (1 - zh) + (hz - 1 - d) * zh for d in range(hz)]
        return near, far


def kernel(lay, experts, tok_in, ids_in, rw_in, wg_in, wu_in, wd_in, sg_in, su_in, sd_in, out,
           tok, part, ids, rw, recvp, recvb0, recvb1, recva0, recva1, recvz0, recvz1, xs, hid, hs,
           wg, wu, wd, sg, su, sd, load_sem, tok_send, tok_recv, red_send, red_recv):
    nz, ny, nt = lay.nz, lay.ny, lay.n_tensor
    rows, half = lay.rows, lay.half
    width = part.shape[-1]
    e_idx, t, p = lax.axis_index("expert"), lax.axis_index("tensor"), lax.axis_index("pair")
    z, y = e_idx // ny, e_idx % ny

    def device(z_, y_, t_):
        return {"expert": z_ * ny + y_, "tensor": t_, "pair": p}

    partner = {"expert": e_idx, "tensor": t, "pair": 1 - p}
    t_peers = [(t + d) % nt for d in range(1, nt)]
    y_peers = [(y + d) % ny for d in range(1, ny)]
    z_peers = [(z + d) % nz for d in range(1, nz)]

    def place(q, z_, y_, t_):
        return ((q * nz + z_) * ny + y_) * nt + t_

    cut = width // 256 * 128
    wide = (pl.ds(0, cut), pl.ds(cut, tok.shape[-1] - cut))
    cols2 = (pl.ds(0, cut), pl.ds(cut, width - cut))
    first_peers, last_peers = (t_peers, y_peers), (y_peers, t_peers)
    first_at, last_at = (t, y), (y, t)

    def yt(h, first_, last_):
        return (last_, first_) if h == 0 else (first_, last_)

    own = place(p, z, y, t)
    first = pltpu.make_async_copy(tok_in, tok.at[own, :, pl.ds(0, width)], load_sem.at[6])
    first.start()
    small = [pltpu.make_async_copy(ids_in, ids, load_sem.at[7]), pltpu.make_async_copy(rw_in, rw, load_sem.at[8])]
    for load in small:
        load.start()
    loads = [
        pltpu.make_async_copy(src, dst, load_sem.at[i])
        for i, (src, dst) in enumerate(
            ((sg_in, sg), (su_in, su), (sd_in, sd), (wg_in.at[0], wg), (wu_in.at[0], wu), (wd_in.at[0], wd))
        )
    ]
    for load in loads:
        load.start()

    barrier = pltpu.get_barrier_semaphore()

    def greet(dev):
        pl.semaphore_signal(barrier, inc=1, device_id=dev, device_id_type=MESH)

    greet(partner)
    for t_ in t_peers:
        greet(device(z, y, t_))
    for y_ in y_peers:
        greet(device(z, y_, t))
    for z_ in z_peers:
        greet(device(z_, y, t))

    for load in small:
        load.wait()
    lane = lax.broadcasted_iota(jnp.int32, (rows, tok.shape[-1] - width), 1)
    top = ids.shape[1]
    pieces = [jnp.zeros(lane.shape, F32) for _ in range(3)]
    for k in range(top):
        for m in range(3):
            pieces[m] = pieces[m] + jnp.where(lane == ids[:, k : k + 1] + m * experts, rw[:, k : k + 1], 0.0)
    hi = [v.astype(BF16).astype(F32) for v in pieces]
    rest = [v - h for v, h in zip(pieces, hi)]
    mid = [v.astype(BF16).astype(F32) for v in rest]
    low = [v - h for v, h in zip(rest, mid)]
    tok[own, :, pl.ds(width, lane.shape[1])] = (hi[0] + mid[1] + low[2]).astype(BF16)

    pl.semaphore_wait(barrier, nt + ny + nz - 2)

    first.wait()

    sent = []

    def both(c1, c2):
        return c2 if c1 is None else (c1 if c2 is None else jnp.logical_and(c1, c2))

    def run(cond, fn):
        if cond is None:
            fn()
        else:
            pl.when(cond)(fn)

    def send(src, dst, sem_send, sem_recv, dev, cond=None):
        copy = pltpu.make_async_remote_copy(
            src_ref=src, dst_ref=dst, send_sem=sem_send, recv_sem=sem_recv,
            device_id=dev, device_id_type=MESH)
        run(cond, copy.start)
        sent.append((cond, copy))

    counter = [0]

    def send_block(h, idx, dev):
        view = tok.at[idx, :, wide[h]]
        send(view, view, tok_send.at[counter[0]], tok_recv.at[h, idx], dev)
        counter[0] += 1

    def arrive(h, idx):
        view = tok.at[idx, :, wide[h]]
        pltpu.make_async_remote_copy(
            src_ref=view, dst_ref=view, send_sem=tok_send.at[0],
            recv_sem=tok_recv.at[h, idx], device_id=partner, device_id_type=MESH).wait_recv()

    near, far = lay.near_far(z)

    def last_sends(h, idx, f):
        for v in last_peers[h]:
            send_block(h, idx, device(z, *yt(h, f, v)))
        send_block(h, idx, partner)

    def line_sends(h, idx):
        for z_ in near[1:] + far:
            send_block(h, idx, device(z_, y, t))

    for h in range(2):
        for f in first_peers[h]:
            send_block(h, own, device(z, *yt(h, f, last_at[h])))
    for h in range(2):
        line_sends(h, own)
    for h in range(2):
        last_sends(h, own, first_at[h])
    for d in range(max(ny, nt) - 1):
        for h in range(2):
            if d < len(first_peers[h]):
                blk = place(p, z, *yt(h, first_peers[h][d], last_at[h]))
                arrive(h, blk)
                line_sends(h, blk)
                last_sends(h, blk, first_at[h])

    def stage_line(z_):
        for d in range(max(ny, nt)):
            for h in range(2):
                firsts = [first_at[h]] + first_peers[h]
                if d < len(firsts):
                    blk = place(p, z_, *yt(h, firsts[d], last_at[h]))
                    arrive(h, blk)
                    last_sends(h, blk, first_at[h])

    def stage_last(z_):
        for h in range(2):
            for f in [first_at[h]] + first_peers[h]:
                for v in last_peers[h]:
                    blk = place(p, z_, *yt(h, f, v))
                    arrive(h, blk)
                    send_block(h, blk, partner)

    def stage_partner(z_):
        for y_ in range(ny):
            for t_ in range(nt):
                for h in range(2):
                    arrive(h, place(1 - p, z_, y_, t_))

    for z_ in near[1:]:
        stage_line(z_)
    for z_ in near:
        stage_last(z_)
    for z_ in far:
        stage_line(z_)
    for z_ in near:
        stage_partner(z_)

    group = []
    for q in range(2):
        for t_ in range(lay.n_tensor):
            group.append(place(q, z, y, t_))
    for i, idx in enumerate(group):
        xs[i] = tok[idx, :, pl.ds(0, width)]
    count = len(group)

    def hidden_tiles(x, w1, w2, scale, store):
        tile = tile_of(w1.shape[1], 256)

        def body(n, _):
            cols = pl.ds(pl.multiple_of(n * tile, tile), tile)
            g = jnp.dot(x(), w1[:, cols], preferred_element_type=F32)
            u = jnp.dot(x(), w2[:, cols], preferred_element_type=F32)
            h = g / (1.0 + jnp.exp(-g)) * u
            if scale is not None:
                h = h * scale
            store[:, cols] = h.astype(BF16)
            return 0

        lax.fori_loop(0, w1.shape[1] // tile, body, 0)

    out_tile = tile_of(width, 512)
    span = half * len(near) // nz
    per = part_rows(span, rows)
    mine = e_idx * lay.n_pair + p

    def rows_of(at):
        extra = tok[pl.ds(at, per), :, pl.ds(width, lane.shape[1])].reshape(per * rows, lane.shape[1])
        l2 = lax.broadcasted_iota(jnp.int32, extra.shape, 1)
        pick = (l2 == mine) | (l2 == mine + experts) | (l2 == mine + 2 * experts)
        scale = jnp.sum(jnp.where(pick, extra.astype(F32), 0.0), axis=1, keepdims=True)
        hidden_tiles(lambda: tok[pl.ds(at, per), :, pl.ds(0, width)].reshape(per * rows, width), wg, wu, scale, hid)

        def body(n, _):
            cols = pl.ds(pl.multiple_of(n * out_tile, out_tile), out_tile)
            v = jnp.dot(hid[...], wd[:, cols], preferred_element_type=F32)
            part[pl.ds(at, per), :, cols] = v.astype(BF16).reshape(per, rows, out_tile)
            return 0

        lax.fori_loop(0, width // out_tile, body, 0)

    def shared_into(q):
        lo = q * (count // 2)

        def body(n, _):
            cols = pl.ds(pl.multiple_of(n * out_tile, out_tile), out_tile)
            r0 = pl.multiple_of(lo * rows, rows)
            v = jnp.dot(hs[pl.ds(r0, count // 2 * rows), :], sd[:, cols], preferred_element_type=F32)
            for j in range(count // 2):
                idx = place(q, z, y, j)
                part[idx, :, cols] = (part[idx, :, cols].astype(F32) + v[j * rows : (j + 1) * rows]).astype(BF16)
            return 0

        lax.fori_loop(0, width // out_tile, body, 0)

    rcount = [0]

    def send_sum(src, dst, recv_at, dev, cond=None):
        send(src, dst, red_send.at[rcount[0]], red_recv.at[recv_at], dev, cond)
        rcount[0] += 1

    def got(dst, recv_at, cond=None):
        copy = pltpu.make_async_remote_copy(
            src_ref=dst, dst_ref=dst, send_sem=red_send.at[0], recv_sem=red_recv.at[recv_at],
            device_id=partner, device_id_type=MESH)
        run(cond, copy.wait_recv)

    steps = span // per
    other = 1 - p

    def compute(q, z_first):
        at0 = place(q, z_first, 0, 0)

        def go(c, _):
            rows_of(at0 + c * per)
            return 0

        lax.fori_loop(0, steps, go, 0)

    def partner_sums(zs):
        for z_ in zs:
            for y_ in range(ny):
                at_ = z_ * ny + y_
                send_sum(part.at[pl.ds(place(other, z_, y_, 0), nt)], recvp.at[pl.ds(at_ * nt, nt)], at_, partner)

    recvb, recva, recvz = (recvb0, recvb1), (recva0, recva1), (recvz0, recvz1)
    base = [half]
    bases = {}

    def at(kind, h, n):
        if (kind, h) not in bases:
            bases[kind, h] = base[0]
            base[0] += n
        return bases[kind, h]

    def buf_b(h, d, z_, f):
        n = lay.first[h]
        at_ = (d * nz + z_) * n + f
        return recvb[h].at[at_], at("b", h, (lay.last[h] - 1) * nz * n) + at_

    def buf_a(h, d):
        return recva[h].at[d], at("a", h, lay.first[h] - 1) + d

    def buf_z(h, d, f):
        n = lay.first[h]
        return recvz[h].at[d * n + f], at("z", h, (nz - 1) * n) + d * n + f

    def add_into(h, idx, others):
        v = part[idx, :, cols2[h]].astype(F32)
        for ref in others:
            v = v + ref[...].astype(F32)
        part[idx, :, cols2[h]] = v.astype(BF16)

    def mine_of(z_, y_, t_, h):
        return recvp.at[(z_ * ny + y_) * nt + t_, :, cols2[h]]

    def sums_last(z_):
        for y_ in range(ny):
            got(recvp.at[pl.ds((z_ * ny + y_) * nt, nt)], z_ * ny + y_)
        for f in range(max(ny, nt) - 1, -1, -1):
            for h in range(2):
                firsts = first_peers[h] + [first_at[h]]
                if f >= len(firsts):
                    continue
                for d, v in enumerate(last_peers[h]):
                    y_, t_ = yt(h, firsts[f], v)
                    idx = place(p, z_, y_, t_)
                    add_into(h, idx, [mine_of(z_, y_, t_, h)])
                    ref, sem = buf_b(h, d, z_, firsts[f])
                    y2, t2 = yt(h, first_at[h], v)
                    send_sum(part.at[idx, :, cols2[h]], ref, sem, device(z, y2, t2))

    def collect_last(h, z_, f):
        y_, t_ = yt(h, f, last_at[h])
        refs = [mine_of(z_, y_, t_, h)]
        for d in range(lay.last[h] - 1):
            ref, sem = buf_b(h, d, z_, f)
            got(ref, sem)
            refs.append(ref)
        return place(p, z_, y_, t_), refs

    def sums_line(z_):
        for f in range(max(ny, nt) - 1, -1, -1):
            for h in range(2):
                firsts = first_peers[h] + [first_at[h]]
                if f >= len(firsts):
                    continue
                idx, refs = collect_last(h, z_, firsts[f])
                add_into(h, idx, refs)
                ref, sem = buf_z(h, (z_ - z + nz) % nz - 1, firsts[f])
                send_sum(part.at[idx, :, cols2[h]], ref, sem, device(z_, y, t))

    def collect_line(h, f):
        idx, refs = collect_last(h, z, f)
        for d in range(nz - 1):
            ref, sem = buf_z(h, d, f)
            got(ref, sem)
            refs.append(ref)
        return idx, refs

    for i in range(3, 6):
        loads[i].wait()
    compute(0, near[0] // len(near) * len(near))
    compute(1, near[0] // len(near) * len(near))
    loads[0].wait()
    loads[1].wait()
    hidden_tiles(lambda: xs[...].reshape(count * rows, width), sg, su, None, hs)
    loads[2].wait()
    shared_into(0)
    shared_into(1)
    partner_sums(near[::-1])
    if far:
        for z_ in far:
            stage_last(z_)
        for z_ in far:
            stage_partner(z_)
        far_first = (1 - near[0] // len(near)) * len(near)
        compute(other, far_first)
        partner_sums(far[::-1])
        for z_ in near[::-1]:
            sums_last(z_)
        compute(p, far_first)
        for z_ in far[::-1]:
            sums_last(z_)
    else:
        for z_ in near[::-1]:
            sums_last(z_)
    for z_ in near[:0:-1] + far[::-1]:
        sums_line(z_)
    for h in range(2):
        for d, f in enumerate(first_peers[h]):
            idx, refs = collect_line(h, f)
            add_into(h, idx, refs)
            ref, sem = buf_a(h, d)
            send_sum(part.at[idx, :, cols2[h]], ref, sem, device(z, *yt(h, f, last_at[h])))
    for h in range(2):
        idx, refs = collect_line(h, first_at[h])
        for d in range(lay.first[h] - 1):
            ref, sem = buf_a(h, d)
            got(ref, sem)
            refs.append(ref)
        add_into(h, idx, refs)
    total = part[own]
    out[...] = total
    for cond, copy in sent:
        run(cond, copy.wait_send)


def per_device(lay, experts, tokens, ids, rw, wg, wu, wd, sg, su, sd):
    rows, width = tokens.shape
    nz, ny, nt = lay.nz, lay.ny, lay.n_tensor
    cut = width // 256 * 128
    count = 2 * lay.n_tensor
    hidden, shared = wg.shape[2], sg.shape[1]
    per = part_rows(lay.half // (1 if nz % 2 else 2), rows)
    sends = 2 * (nt + ny) * nz + 4 * nz * nt * ny
    red = nz * ny + 2 * nz * nt * ny + (nz + 1) * (nt + ny)
    halves = (cut, width - cut)
    many_b = [max(1, (lay.last[h] - 1) * nz * lay.first[h]) for h in range(2)]
    many_a = [max(1, lay.first[h] - 1) for h in range(2)]
    many_z = [max(1, (nz - 1) * lay.first[h]) for h in range(2)]
    vmem = pl.BlockSpec(memory_space=pltpu.VMEM)
    anyw = pl.BlockSpec(memory_space=pl.ANY)
    scratch = [
        pltpu.VMEM((lay.blocks, rows, width + lanes_for(experts)), BF16),
        pltpu.VMEM((lay.blocks, rows, width), BF16),
        pltpu.VMEM(ids.shape, jnp.int32),
        pltpu.VMEM(rw.shape, F32),
        pltpu.VMEM((lay.half, rows, width), BF16),
        pltpu.VMEM((many_b[0], rows, halves[0]), BF16),
        pltpu.VMEM((many_b[1], rows, halves[1]), BF16),
        pltpu.VMEM((many_a[0], rows, halves[0]), BF16),
        pltpu.VMEM((many_a[1], rows, halves[1]), BF16),
        pltpu.VMEM((many_z[0], rows, halves[0]), BF16),
        pltpu.VMEM((many_z[1], rows, halves[1]), BF16),
        pltpu.VMEM((count, rows, width), BF16),
        pltpu.VMEM((per * rows, hidden), BF16),
        pltpu.VMEM((count * rows, shared), BF16),
        pltpu.VMEM(wg.shape[1:], BF16),
        pltpu.VMEM(wu.shape[1:], BF16),
        pltpu.VMEM(wd.shape[1:], BF16),
        pltpu.VMEM(sg.shape, BF16),
        pltpu.VMEM(su.shape, BF16),
        pltpu.VMEM(sd.shape, BF16),
        pltpu.SemaphoreType.DMA((9,)),
        pltpu.SemaphoreType.DMA((sends,)),
        pltpu.SemaphoreType.DMA((2, lay.blocks)),
        pltpu.SemaphoreType.DMA((red,)),
        pltpu.SemaphoreType.DMA((lay.half + sum(many_b) + sum(many_a) + sum(many_z),)),
    ]
    return pl.pallas_call(
        functools.partial(kernel, lay, experts),
        out_shape=jax.ShapeDtypeStruct((rows, width), BF16),
        in_specs=[anyw] * 9,
        out_specs=vmem,
        scratch_shapes=scratch,
        compiler_params=pltpu.CompilerParams(
            collective_id=0, has_side_effects=True, vmem_limit_bytes=67043328
        ),
    )(tokens, ids, rw, wg, wu, wd, sg, su, sd)


def solution(mesh):
    shape = dict(mesh.shape)

    def body(tokens, ids, rw, wg, wu, wd, sg, su, sd):
        lay = Layout(shape["expert"], shape["tensor"], shape["pair"], tokens.shape[0])
        experts = shape["expert"] * shape["pair"] * wg.shape[0]
        return per_device(lay, experts, tokens, ids, rw, wg, wu, wd, sg, su, sd)

    in_specs = (
        P(("groups", "expert", "tensor", "pair"), None),
        P(("groups", "expert", "tensor", "pair"), None),
        P(("groups", "expert", "tensor", "pair"), None),
        P(("expert", "pair"), None, "tensor"),
        P(("expert", "pair"), None, "tensor"),
        P(("expert", "pair"), "tensor", None),
        P(None, ("tensor", "pair")),
        P(None, ("tensor", "pair")),
        P(("tensor", "pair"), None),
    )
    out_specs = P(("groups", "expert", "tensor", "pair"), None)
    return jax.shard_map(body, mesh=mesh, in_specs=in_specs, out_specs=out_specs, check_vma=False)
```

```python
import functools

import jax
import jax.numpy as jnp
from jax import lax
from jax.experimental import pallas as pl
from jax.experimental.pallas import tpu as pltpu
from jax.sharding import PartitionSpec as P

MESH = pl.DeviceIdType.MESH
F32 = jnp.float32
BF16 = jnp.bfloat16


def lanes_for(experts):
    return -(-3 * experts // 128) * 128


def tile_of(width, most):
    for tile in range(min(width, most), 0, -1):
        if width % tile == 0 and (tile % 128 == 0 or tile == width):
            return tile
    return width


def part_rows(span, rows):
    per = min(span, max(1, 256 // rows))
    while span % per:
        per -= 1
    return per


class Layout:
    def __init__(self, n_expert, n_tensor, n_pair, tok_rows):
        self.n_expert, self.n_tensor, self.n_pair = n_expert, n_tensor, n_pair
        self.ny = 2 if n_expert % 2 == 0 else 1
        self.nz = n_expert // self.ny
        self.half = n_expert * n_tensor
        self.blocks = 2 * self.half
        self.rows = tok_rows
        self.first = (n_tensor, self.ny)
        self.last = (self.ny, n_tensor)

    def near_far(self, z):
        if self.nz % 2:
            return [z] + [(z + d) % self.nz for d in range(1, self.nz)], []
        hz = self.nz // 2
        zh = z // hz
        near = [z] + [zh * hz + (z + d) % hz for d in range(1, hz)]
        far = [(hz + d) * (1 - zh) + (hz - 1 - d) * zh for d in range(hz)]
        return near, far


def kernel(lay, experts, tok_in, ids, rw, wg_in, wu_in, wd_in, sg_in, su_in, sd_in, out,
           tok, part, recvp, recvb0, recvb1, recva0, recva1, recvz0, recvz1, xs, hid, hs,
           wg, wu, wd, sg, su, sd, load_sem, tok_send, tok_recv, red_send, red_recv):
    nz, ny, nt = lay.nz, lay.ny, lay.n_tensor
    rows, half = lay.rows, lay.half
    width = part.shape[-1]
    e_idx, t, p = lax.axis_index("expert"), lax.axis_index("tensor"), lax.axis_index("pair")
    z, y = e_idx // ny, e_idx % ny

    def device(z_, y_, t_):
        return {"expert": z_ * ny + y_, "tensor": t_, "pair": p}

    partner = {"expert": e_idx, "tensor": t, "pair": 1 - p}
    t_peers = [(t + d) % nt for d in range(1, nt)]
    y_peers = [(y + d) % ny for d in range(1, ny)]

    def place(q, z_, y_, t_):
        return ((q * nz + z_) * ny + y_) * nt + t_

    cut = width // 256 * 128
    wide = (pl.ds(0, cut), pl.ds(cut, tok.shape[-1] - cut))
    cols2 = (pl.ds(0, cut), pl.ds(cut, width - cut))
    first_peers, last_peers = (t_peers, y_peers), (y_peers, t_peers)
    first_at, last_at = (t, y), (y, t)

    def yt(h, first_, last_):
        return (last_, first_) if h == 0 else (first_, last_)

    own = place(p, z, y, t)
    first = pltpu.make_async_copy(tok_in, tok.at[own, :, pl.ds(0, width)], load_sem.at[6])
    first.start()
    loads = [
        pltpu.make_async_copy(src, dst, load_sem.at[i])
        for i, (src, dst) in enumerate(
            ((sg_in, sg), (su_in, su), (sd_in, sd), (wg_in.at[0], wg), (wu_in.at[0], wu), (wd_in.at[0], wd))
        )
    ]
    for load in loads:
        load.start()

    barrier = pltpu.get_barrier_semaphore()

    def greet(dev):
        pl.semaphore_signal(barrier, inc=1, device_id=dev, device_id_type=MESH)

    greet(partner)
    for t_ in t_peers:
        greet(device(z, y, t_))
    for y_ in y_peers:
        greet(device(z, y_, t))

    @pl.when(z < nz - 1)
    def _():
        greet(device(z + 1, y, t))

    @pl.when(z > 0)
    def _():
        greet(device(z - 1, y, t))

    lane = lax.broadcasted_iota(jnp.int32, (rows, tok.shape[-1] - width), 1)
    top = ids.shape[1]
    pieces = [jnp.zeros(lane.shape, F32) for _ in range(3)]
    for k in range(top):
        for m in range(3):
            pieces[m] = pieces[m] + jnp.where(lane == ids[:, k : k + 1] + m * experts, rw[:, k : k + 1], 0.0)
    hi = [v.astype(BF16).astype(F32) for v in pieces]
    rest = [v - h for v, h in zip(pieces, hi)]
    mid = [v.astype(BF16).astype(F32) for v in rest]
    low = [v - h for v, h in zip(rest, mid)]
    tok[own, :, pl.ds(width, lane.shape[1])] = (hi[0] + mid[1] + low[2]).astype(BF16)

    pl.semaphore_wait(barrier, nt + ny - 1 + jnp.minimum(z, 1) + jnp.minimum(nz - 1 - z, 1))

    first.wait()

    sent = []

    def both(c1, c2):
        return c2 if c1 is None else (c1 if c2 is None else jnp.logical_and(c1, c2))

    def run(cond, fn):
        if cond is None:
            fn()
        else:
            pl.when(cond)(fn)

    def send(src, dst, sem_send, sem_recv, dev, cond=None):
        copy = pltpu.make_async_remote_copy(
            src_ref=src, dst_ref=dst, send_sem=sem_send, recv_sem=sem_recv,
            device_id=dev, device_id_type=MESH)
        run(cond, copy.start)
        sent.append((cond, copy))

    counter = [0]

    def send_block(h, idx, dev, cond=None):
        view = tok.at[idx, :, wide[h]]
        send(view, view, tok_send.at[counter[0]], tok_recv.at[h, idx], dev, cond)
        counter[0] += 1

    def arrive(h, idx):
        view = tok.at[idx, :, wide[h]]
        pltpu.make_async_remote_copy(
            src_ref=view, dst_ref=view, send_sem=tok_send.at[0],
            recv_sem=tok_recv.at[h, idx], device_id=partner, device_id_type=MESH).wait_recv()

    near, far = lay.near_far(z)

    def last_sends(h, idx, f):
        for v in last_peers[h]:
            send_block(h, idx, device(z, *yt(h, f, v)))
        send_block(h, idx, partner)

    def line_sends(h, idx):
        send_block(h, idx, device(z + 1, y, t), z < nz - 1)
        send_block(h, idx, device(z - 1, y, t), z > 0)

    def onward(h, idx, z_):
        way = 2 * jnp.minimum(jnp.maximum(z - z_, 0), 1) - 1
        to = z + way
        send_block(h, idx, device(to, y, t), jnp.logical_and(to >= 0, to < nz))

    for h in range(2):
        for f in first_peers[h]:
            send_block(h, own, device(z, *yt(h, f, last_at[h])))
    for h in range(2):
        line_sends(h, own)
    for h in range(2):
        last_sends(h, own, first_at[h])
    for d in range(max(ny, nt) - 1):
        for h in range(2):
            if d < len(first_peers[h]):
                blk = place(p, z, *yt(h, first_peers[h][d], last_at[h]))
                arrive(h, blk)
                line_sends(h, blk)
                last_sends(h, blk, first_at[h])

    def stage_line(z_):
        for d in range(max(ny, nt)):
            for h in range(2):
                firsts = [first_at[h]] + first_peers[h]
                if d < len(firsts):
                    blk = place(p, z_, *yt(h, firsts[d], last_at[h]))
                    arrive(h, blk)
                    onward(h, blk, z_)
                    last_sends(h, blk, first_at[h])

    def stage_last(z_):
        for h in range(2):
            for f in [first_at[h]] + first_peers[h]:
                for v in last_peers[h]:
                    blk = place(p, z_, *yt(h, f, v))
                    arrive(h, blk)
                    send_block(h, blk, partner)

    def stage_partner(z_):
        for y_ in range(ny):
            for t_ in range(nt):
                for h in range(2):
                    arrive(h, place(1 - p, z_, y_, t_))

    for z_ in near[1:]:
        stage_line(z_)
    for z_ in near:
        stage_last(z_)
    for z_ in far:
        stage_line(z_)
    for z_ in near:
        stage_partner(z_)

    group = []
    for q in range(2):
        for t_ in range(lay.n_tensor):
            group.append(place(q, z, y, t_))
    for i, idx in enumerate(group):
        xs[i] = tok[idx, :, pl.ds(0, width)]
    count = len(group)

    def hidden_tiles(x, w1, w2, scale, store):
        tile = tile_of(w1.shape[1], 256)

        def body(n, _):
            cols = pl.ds(pl.multiple_of(n * tile, tile), tile)
            g = jnp.dot(x(), w1[:, cols], preferred_element_type=F32)
            u = jnp.dot(x(), w2[:, cols], preferred_element_type=F32)
            h = g / (1.0 + jnp.exp(-g)) * u
            if scale is not None:
                h = h * scale
            store[:, cols] = h.astype(BF16)
            return 0

        lax.fori_loop(0, w1.shape[1] // tile, body, 0)

    out_tile = tile_of(width, 512)
    span = half * len(near) // nz
    per = part_rows(span, rows)
    mine = e_idx * lay.n_pair + p

    def rows_of(at):
        extra = tok[pl.ds(at, per), :, pl.ds(width, lane.shape[1])].reshape(per * rows, lane.shape[1])
        l2 = lax.broadcasted_iota(jnp.int32, extra.shape, 1)
        pick = (l2 == mine) | (l2 == mine + experts) | (l2 == mine + 2 * experts)
        scale = jnp.sum(jnp.where(pick, extra.astype(F32), 0.0), axis=1, keepdims=True)
        hidden_tiles(lambda: tok[pl.ds(at, per), :, pl.ds(0, width)].reshape(per * rows, width), wg, wu, scale, hid)

        def body(n, _):
            cols = pl.ds(pl.multiple_of(n * out_tile, out_tile), out_tile)
            v = jnp.dot(hid[...], wd[:, cols], preferred_element_type=F32)
            part[pl.ds(at, per), :, cols] = v.astype(BF16).reshape(per, rows, out_tile)
            return 0

        lax.fori_loop(0, width // out_tile, body, 0)

    def shared_into(q):
        lo = q * (count // 2)

        def body(n, _):
            cols = pl.ds(pl.multiple_of(n * out_tile, out_tile), out_tile)
            r0 = pl.multiple_of(lo * rows, rows)
            v = jnp.dot(hs[pl.ds(r0, count // 2 * rows), :], sd[:, cols], preferred_element_type=F32)
            for j in range(count // 2):
                idx = place(q, z, y, j)
                part[idx, :, cols] = (part[idx, :, cols].astype(F32) + v[j * rows : (j + 1) * rows]).astype(BF16)
            return 0

        lax.fori_loop(0, width // out_tile, body, 0)

    rcount = [0]

    def send_sum(src, dst, recv_at, dev, cond=None):
        send(src, dst, red_send.at[rcount[0]], red_recv.at[recv_at], dev, cond)
        rcount[0] += 1

    def got(dst, recv_at, cond=None):
        copy = pltpu.make_async_remote_copy(
            src_ref=dst, dst_ref=dst, send_sem=red_send.at[0], recv_sem=red_recv.at[recv_at],
            device_id=partner, device_id_type=MESH)
        run(cond, copy.wait_recv)

    steps = span // per
    other = 1 - p

    def compute(q, z_first):
        at0 = place(q, z_first, 0, 0)

        def go(c, _):
            rows_of(at0 + c * per)
            return 0

        lax.fori_loop(0, steps, go, 0)

    def partner_sums(zs):
        for z_ in zs:
            for y_ in range(ny):
                at_ = z_ * ny + y_
                send_sum(part.at[pl.ds(place(other, z_, y_, 0), nt)], recvp.at[pl.ds(at_ * nt, nt)], at_, partner)

    recvb, recva, recvz = (recvb0, recvb1), (recva0, recva1), (recvz0, recvz1)
    base = [half]
    bases = {}

    def at(kind, h, n):
        if (kind, h) not in bases:
            bases[kind, h] = base[0]
            base[0] += n
        return bases[kind, h]

    def buf_b(h, d, z_, f):
        n = lay.first[h]
        at_ = (d * nz + z_) * n + f
        return recvb[h].at[at_], at("b", h, (lay.last[h] - 1) * nz * n) + at_

    def buf_a(h, d):
        return recva[h].at[d], at("a", h, lay.first[h] - 1) + d

    def buf_z(h, slot, f):
        n = lay.first[h]
        return recvz[h].at[slot * n + f], at("z", h, (nz + 1) * n) + slot * n + f

    def add_into(h, idx, others):
        v = part[idx, :, cols2[h]].astype(F32)
        for ref in others:
            v = v + ref[...].astype(F32)
        part[idx, :, cols2[h]] = v.astype(BF16)

    def mine_of(z_, y_, t_, h):
        return recvp.at[(z_ * ny + y_) * nt + t_, :, cols2[h]]

    def sums_last(z_):
        for y_ in range(ny):
            got(recvp.at[pl.ds((z_ * ny + y_) * nt, nt)], z_ * ny + y_)
        for f in range(max(ny, nt) - 1, -1, -1):
            for h in range(2):
                firsts = first_peers[h] + [first_at[h]]
                if f >= len(firsts):
                    continue
                for d, v in enumerate(last_peers[h]):
                    y_, t_ = yt(h, firsts[f], v)
                    idx = place(p, z_, y_, t_)
                    add_into(h, idx, [mine_of(z_, y_, t_, h)])
                    ref, sem = buf_b(h, d, z_, firsts[f])
                    y2, t2 = yt(h, first_at[h], v)
                    send_sum(part.at[idx, :, cols2[h]], ref, sem, device(z, y2, t2))

    def collect_last(h, z_, f):
        y_, t_ = yt(h, f, last_at[h])
        refs = [mine_of(z_, y_, t_, h)]
        for d in range(lay.last[h] - 1):
            ref, sem = buf_b(h, d, z_, f)
            got(ref, sem)
            refs.append(ref)
        return place(p, z_, y_, t_), refs

    def sums_line(z_):
        gt = jnp.minimum(jnp.maximum(z_ - z, 0), 1)
        way, slot = 2 * gt - 1, z_ + gt
        back = z - way
        inner = jnp.logical_and(back >= 0, back < nz)
        for f in range(max(ny, nt) - 1, -1, -1):
            for h in range(2):
                firsts = first_peers[h] + [first_at[h]]
                if f >= len(firsts):
                    continue
                idx, refs = collect_last(h, z_, firsts[f])
                ref, sem = buf_z(h, slot, firsts[f])
                got(ref, sem, inner)
                chain_add(h, idx, refs, ref, inner)
                send_sum(part.at[idx, :, cols2[h]], ref, sem, device(z + way, y, t))

    def chain_add(h, idx, refs, ref, inner):
        @pl.when(inner)
        def _():
            add_into(h, idx, refs + [ref])

        @pl.when(jnp.logical_not(inner))
        def _():
            add_into(h, idx, refs)

    def collect_line(h, f):
        idx, refs = collect_last(h, z, f)
        for slot, cond in ((z + 1, z > 0), (z, z < nz - 1)):
            ref, sem = buf_z(h, slot, f)
            got(ref, sem, cond)

            @pl.when(cond)
            def _(ref=ref):
                add_into(h, idx, [ref])
        return idx, refs

    for i in range(3, 6):
        loads[i].wait()
    compute(0, near[0] // len(near) * len(near))
    compute(1, near[0] // len(near) * len(near))
    loads[0].wait()
    loads[1].wait()
    hidden_tiles(lambda: xs[...].reshape(count * rows, width), sg, su, None, hs)
    loads[2].wait()
    shared_into(0)
    shared_into(1)
    partner_sums(near[::-1])
    if far:
        for z_ in far:
            stage_last(z_)
        for z_ in far:
            stage_partner(z_)
        far_first = (1 - near[0] // len(near)) * len(near)
        compute(other, far_first)
        partner_sums(far[::-1])
        for z_ in near[::-1]:
            sums_last(z_)
        compute(p, far_first)
        for z_ in far[::-1]:
            sums_last(z_)
    else:
        for z_ in near[::-1]:
            sums_last(z_)
    for z_ in far[::-1] + near[:0:-1]:
        sums_line(z_)
    for h in range(2):
        for d, f in enumerate(first_peers[h]):
            idx, refs = collect_line(h, f)
            add_into(h, idx, refs)
            ref, sem = buf_a(h, d)
            send_sum(part.at[idx, :, cols2[h]], ref, sem, device(z, *yt(h, f, last_at[h])))
    for h in range(2):
        idx, refs = collect_line(h, first_at[h])
        for d in range(lay.first[h] - 1):
            ref, sem = buf_a(h, d)
            got(ref, sem)
            refs.append(ref)
        add_into(h, idx, refs)
    total = part[own]
    out[...] = total
    for cond, copy in sent:
        run(cond, copy.wait_send)


def per_device(lay, experts, tokens, ids, rw, wg, wu, wd, sg, su, sd):
    rows, width = tokens.shape
    nz, ny, nt = lay.nz, lay.ny, lay.n_tensor
    cut = width // 256 * 128
    count = 2 * lay.n_tensor
    hidden, shared = wg.shape[2], sg.shape[1]
    per = part_rows(lay.half // (1 if nz % 2 else 2), rows)
    sends = 2 * (nt + ny) * nz + 4 * nz * nt * ny
    red = nz * ny + 2 * nz * nt * ny + (nz + 1) * (nt + ny)
    halves = (cut, width - cut)
    many_b = [max(1, (lay.last[h] - 1) * nz * lay.first[h]) for h in range(2)]
    many_a = [max(1, lay.first[h] - 1) for h in range(2)]
    many_z = [(nz + 1) * lay.first[h] for h in range(2)]
    vmem = pl.BlockSpec(memory_space=pltpu.VMEM)
    anyw = pl.BlockSpec(memory_space=pl.ANY)
    scratch = [
        pltpu.VMEM((lay.blocks, rows, width + lanes_for(experts)), BF16),
        pltpu.VMEM((lay.blocks, rows, width), BF16),
        pltpu.VMEM((lay.half, rows, width), BF16),
        pltpu.VMEM((many_b[0], rows, halves[0]), BF16),
        pltpu.VMEM((many_b[1], rows, halves[1]), BF16),
        pltpu.VMEM((many_a[0], rows, halves[0]), BF16),
        pltpu.VMEM((many_a[1], rows, halves[1]), BF16),
        pltpu.VMEM((many_z[0], rows, halves[0]), BF16),
        pltpu.VMEM((many_z[1], rows, halves[1]), BF16),
        pltpu.VMEM((count, rows, width), BF16),
        pltpu.VMEM((per * rows, hidden), BF16),
        pltpu.VMEM((count * rows, shared), BF16),
        pltpu.VMEM(wg.shape[1:], BF16),
        pltpu.VMEM(wu.shape[1:], BF16),
        pltpu.VMEM(wd.shape[1:], BF16),
        pltpu.VMEM(sg.shape, BF16),
        pltpu.VMEM(su.shape, BF16),
        pltpu.VMEM(sd.shape, BF16),
        pltpu.SemaphoreType.DMA((9,)),
        pltpu.SemaphoreType.DMA((sends,)),
        pltpu.SemaphoreType.DMA((2, lay.blocks)),
        pltpu.SemaphoreType.DMA((red,)),
        pltpu.SemaphoreType.DMA((lay.half + sum(many_b) + sum(many_a) + sum(many_z),)),
    ]
    return pl.pallas_call(
        functools.partial(kernel, lay, experts),
        out_shape=jax.ShapeDtypeStruct((rows, width), BF16),
        in_specs=[anyw, vmem, vmem] + [anyw] * 6,
        out_specs=vmem,
        scratch_shapes=scratch,
        compiler_params=pltpu.CompilerParams(
            collective_id=0, has_side_effects=True, vmem_limit_bytes=67043328
        ),
    )(tokens, ids, rw, wg, wu, wd, sg, su, sd)


def solution(mesh):
    shape = dict(mesh.shape)

    def body(tokens, ids, rw, wg, wu, wd, sg, su, sd):
        lay = Layout(shape["expert"], shape["tensor"], shape["pair"], tokens.shape[0])
        experts = shape["expert"] * shape["pair"] * wg.shape[0]
        return per_device(lay, experts, tokens, ids, rw, wg, wu, wd, sg, su, sd)

    in_specs = (
        P(("groups", "expert", "tensor", "pair"), None),
        P(("groups", "expert", "tensor", "pair"), None),
        P(("groups", "expert", "tensor", "pair"), None),
        P(("expert", "pair"), None, "tensor"),
        P(("expert", "pair"), None, "tensor"),
        P(("expert", "pair"), "tensor", None),
        P(None, ("tensor", "pair")),
        P(None, ("tensor", "pair")),
        P(("tensor", "pair"), None),
    )
    out_specs = P(("groups", "expert", "tensor", "pair"), None)
    return jax.shard_map(body, mesh=mesh, in_specs=in_specs, out_specs=out_specs, check_vma=False)
```
